128 devices in a mesh: section: 8 (over y_hi, z), seq: 16 (over x, y_lo, core).
Axes of the slice: x: 4, y: 4 (y_hi: 2, y_lo: 2; y = y_hi * 2 + y_lo), z: 4, core: 2. Of those that a mesh axis runs over, the one named last changes fastest.
Arguments:
- inbound_embedding_batches: bfloat16 [2, 128, 4096], replicated, may hold values from -16 to 16
- decoder_embedding_batches: bfloat16 [2, 128, 4096], replicated, may hold values from -16 to 16
- asking_projections: bfloat16 [8, 4096, 4096], P('section', None, 'seq'), may hold values from -0.09375 to 0.09375
- probe_projections: bfloat16 [8, 4096, 4096], P('section', None, 'seq'), may hold values from -0.09375 to 0.09375
- payload_projections: bfloat16 [8, 4096, 4096], P('section', None, 'seq'), may hold values from -0.09375 to 0.09375
- exit_projections: bfloat16 [8, 4096, 4096], P('section', 'seq'), may hold values from -0.1875 to 0.1875
- layer_rescale_weights: float32 [8, 4096], P('section'), may hold values from 0.1 to 1.9
- logit_sharpness: float32 [8, 64], P('section', 'seq'), may hold values from 0.5 to 3
- last_rescale_weights: float32 [4096], replicated, may hold values from 0.1 to 1.9
Outputs:
- section_out: bfloat16 [8, 2, 128, 4096], P('section')
The draws below stay inside these ranges and needn't reach their ends.
All inputs are finite; a program needn't handle non-finite values.
Results may differ from the reference program's by a relative error of at most 0.025.
Values may be sent and summed in bfloat16 or wider, within the bound.
A program may use at most 64 MiB of HBM per device.

```python
import math
import jax
import jax.numpy as jnp
from jax import lax

D = 4096
NUM_HEADS = 64
LENGTH = 128
MICRO = 2
INNER = 4096
ENC_SECTIONS = 3
N_SECTION = 8
N_SEQ = 16


def scaled_embeddings(key):
    first_key, second_key, third_key = jax.random.split(key, 3)
    base = jax.random.normal(first_key, (MICRO, LENGTH, D), jnp.float32)
    base = jnp.clip(base, -4.0, 4.0)
    row_scale = jnp.exp(jax.random.uniform(second_key, (MICRO, LENGTH, 1), jnp.float32, math.log(0.2), math.log(2.0)))
    column_scale = jnp.exp(jax.random.uniform(third_key, (1, 1, D), jnp.float32, math.log(0.5), math.log(2.0)))
    return base * row_scale * column_scale


def draw_inbound_embedding_batches(key, part):
    return scaled_embeddings(jax.random.fold_in(key, 11)).astype(jnp.bfloat16)


def draw_decoder_embedding_batches(key, part):
    return scaled_embeddings(jax.random.fold_in(key, 23)).astype(jnp.bfloat16)


def levels(stream_key, shape, shards, least, high):
    def one(position, parts):
        heights = jax.random.uniform(jax.random.fold_in(jax.random.fold_in(stream_key, 6), position), (parts,), jnp.float32, least / len(shards), high / len(shards))
        return jnp.repeat(jnp.exp(heights), shape[position] // parts).reshape((-1,) + (1,) * (len(shape) - position - 1))

    factor_of = one(*shards[0])
    for cut in shards[1:]:
        factor_of = factor_of * one(*cut)
    return factor_of


def noise(key, shape, deviation, reach, shards=(), held_as=jnp.bfloat16):
    loudness = levels(key, shape, shards, -0.22, 0.18) if shards else 1.0
    entries = jax.random.normal(key, shape, jnp.float32) * deviation * loudness
    return jnp.minimum(jnp.maximum(entries, -reach), reach).astype(held_as)


def setup_inputs(seed: int = 0) -> dict:
    key_of = jax.random.split(jax.random.key(seed), 10)
    inbound_embedding_batches = draw_inbound_embedding_batches(jax.random.fold_in(key_of[9], 71), 0)
    decoder_embedding_batches = draw_decoder_embedding_batches(jax.random.fold_in(key_of[9], 71), 0)
    asking_projections = noise(key_of[2], (N_SECTION, D, INNER), D ** -0.5, 0.09375, ((0, 8), (2, 16)))
    probe_projections = noise(key_of[3], (N_SECTION, D, INNER), D ** -0.5, 0.09375, ((0, 8), (2, 16)))
    payload_projections = noise(key_of[4], (N_SECTION, D, INNER), D ** -0.5, 0.09375, ((0, 8), (2, 16)))
    exit_projections = noise(key_of[5], (N_SECTION, INNER, D), (INNER // 4) ** -0.5, 0.1875, ((0, 8), (1, 16)))
    layer_rescale_weights = jnp.clip(1.0 + 0.18 * jax.random.normal(key_of[6], (N_SECTION, D), jnp.float32), 0.1, 1.9)
    logit_sharpness = jnp.clip(jnp.exp(math.log(3.0) - 1.7917595 * jax.random.uniform(key_of[7], (N_SECTION, NUM_HEADS), jnp.float32) ** levels(key_of[7], (N_SECTION, NUM_HEADS), ((0, 8), (1, 16)), -0.2, 0.2)), 0.5, 3.0)
    last_rescale_weights = jnp.clip(1.0 + 0.18 * jax.random.normal(key_of[8], (D,), jnp.float32), 0.1, 1.9)
    return dict(inbound_embedding_batches=inbound_embedding_batches, decoder_embedding_batches=decoder_embedding_batches, asking_projections=asking_projections, probe_projections=probe_projections, payload_projections=payload_projections, exit_projections=exit_projections, layer_rescale_weights=layer_rescale_weights, logit_sharpness=logit_sharpness, last_rescale_weights=last_rescale_weights)


epsilon = 1e-06

def normalize(row_block, gain_vector):
    values = row_block.astype(jnp.float32)
    factor = lax.rsqrt(lax.optimization_barrier(jnp.mean(values * values, axis=-1, keepdims=True)) + epsilon)
    return (values * factor * gain_vector).astype(jnp.bfloat16)

def unit_heads(projected):
    return (projected * lax.rsqrt(lax.optimization_barrier(jnp.mean(projected * projected, axis=-1, keepdims=True)) + epsilon)).astype(jnp.bfloat16)

def mixed_context(rescaled_activations, context_states, w_query, w_key, w_value, logit_divisor):
    length = rescaled_activations.shape[0]
    head_count = logit_divisor.shape[0]
    head_size = w_query.shape[1] // head_count
    queries = jnp.dot(rescaled_activations, w_query, preferred_element_type=jnp.float32).reshape(length, head_count, head_size)
    keys_proj = jnp.dot(context_states, w_key, preferred_element_type=jnp.float32).reshape(context_states.shape[0], head_count, head_size)
    values_proj = jnp.dot(context_states, w_value, preferred_element_type=jnp.float32).astype(jnp.bfloat16)
    values_proj = values_proj.reshape(context_states.shape[0], head_count, head_size)
    unit_query = unit_heads(queries)
    unit_key = unit_heads(keys_proj)
    scores = jnp.einsum('qhd,khd->hqk', unit_query.astype(jnp.float32), unit_key.astype(jnp.float32), precision=lax.Precision.HIGHEST)
    scores = scores * (logit_divisor.astype(jnp.float32)[:, None, None] / math.sqrt(head_size))
    weights = jnp.exp(scores)
    weights = (weights / lax.optimization_barrier(jnp.sum(weights, axis=-1, keepdims=True))).astype(jnp.bfloat16)
    blended_payloads = jnp.einsum('hqk,khd->qhd', weights.astype(jnp.float32), values_proj.astype(jnp.float32), precision=lax.Precision.HIGHEST)
    return blended_payloads.astype(jnp.bfloat16).reshape(length, head_count * head_size)

def project_out(blended_payloads, w_output):
    block = blended_payloads.shape[1] // N_SEQ
    total = jnp.zeros((blended_payloads.shape[0], w_output.shape[1]), jnp.float32)
    for block_index in range(N_SEQ):
        lower = block_index * block
        partial_term = jnp.dot(blended_payloads[:, lower:lower + block], w_output[lower:lower + block], preferred_element_type=jnp.float32).astype(jnp.bfloat16)
        partial_term = lax.optimization_barrier(partial_term)
        total = total + partial_term.astype(jnp.float32)
    return total

def reference(inbound_embedding_batches, decoder_embedding_batches, asking_projections, probe_projections, payload_projections, exit_projections, layer_rescale_weights, logit_sharpness, last_rescale_weights):
    table = []
    for present_layer_index in range(N_SECTION):
        table.append([])
    for batch_index in range(MICRO):
        stream = inbound_embedding_batches[batch_index]
        encoded = stream
        for present_layer_index in range(N_SECTION):
            if present_layer_index == ENC_SECTIONS:
                stream = decoder_embedding_batches[batch_index]
            rescaled_activations = normalize(stream, layer_rescale_weights[present_layer_index])
            if present_layer_index < ENC_SECTIONS:
                context_states = rescaled_activations
            else:
                context_states = normalize(encoded, last_rescale_weights)
            blended_payloads = mixed_context(rescaled_activations, context_states, asking_projections[present_layer_index], probe_projections[present_layer_index], payload_projections[present_layer_index], logit_sharpness[present_layer_index])
            update = project_out(blended_payloads, exit_projections[present_layer_index])
            stream = (stream.astype(jnp.float32) + update).astype(jnp.bfloat16)
            table[present_layer_index].append(stream)
            if present_layer_index == ENC_SECTIONS - 1:
                encoded = stream
    return jnp.stack([jnp.stack(column) for column in table])
```

```python
import functools

import jax
import jax.numpy as jnp
from jax import lax
from jax.experimental import pallas as pl
from jax.experimental.pallas import tpu as pltpu
from jax.sharding import PartitionSpec as P

MESH = pl.DeviceIdType.MESH
EPS = 1e-06
F32 = jnp.float32
BF16 = jnp.bfloat16

RING = 4


def kernel(
    inbound,
    decoder,
    w_query,
    w_key,
    w_value,
    w_out,
    gain,
    sharpness,
    last_gain,
    result,
    weights,
    out_weights,
    x_buf,
    mix_buf,
    mem_buf,
    out_buf,
    q_unit,
    k_unit,
    v_rows,
    acc,
    squares,
    out_acc,
    x_recv,
    mix_recv,
    mem_recv,
    out_recv,
    x_send,
    mix_send,
    mem_send,
    out_send,
    next_send,
    wo_recv,
    wo_send,
    load_sem,
    x_load,
    store_sem,
):
    sections = lax.axis_size("section")
    seq = lax.axis_size("seq")
    encoders = 3 * sections // 8
    section = lax.axis_index("section")
    me = lax.axis_index("seq")
    batches, blocks, length, width = x_buf.shape
    features = blocks * width
    half = length // 2
    heads = sharpness.shape[1]
    head_size = width // heads
    x_pos, y_pos, core = me // 4, (me // 2) % 2, me % 2

    def at(dx, dy, dc):
        return ((x_pos + dx) % RING) * 4 + ((y_pos + dy) % 2) * 2 + (core + dc) % 2

    def columns(j):
        return pl.ds(pl.multiple_of(j * width, width), width)

    loads = [
        pltpu.make_async_copy(
            w_ref.at[0], weights.at[:, pl.ds(i * width, width)], load_sem.at[i]
        )
        for i, w_ref in enumerate((w_query, w_key, w_value))
    ]
    for load in loads:
        load.start()

    def load_x(source):
        for m in range(batches):

            def one(j, carry):
                pltpu.make_async_copy(
                    source.at[m, :, columns(j)], x_buf.at[m, j], x_load.at[m]
                ).start()
                return carry

            lax.fori_loop(0, blocks, one, 0)

    pl.when(section == 0)(lambda: load_x(inbound))
    pl.when(section == encoders)(lambda: load_x(decoder))
    own_wo = pltpu.make_async_copy(w_out.at[0, :, columns(me)], out_weights.at[me], load_sem.at[3])
    own_wo.start()

    barrier = pltpu.get_barrier_semaphore()

    def greet_peer(i, carry):
        pl.semaphore_signal(
            barrier, inc=1, device_id=(section, (me + i) % seq), device_id_type=MESH
        )
        return carry

    def greet_section(i, carry):
        pl.semaphore_signal(
            barrier, inc=1, device_id=((section + i) % sections, me), device_id_type=MESH
        )
        return carry

    lax.fori_loop(1, seq, greet_peer, 0)
    lax.fori_loop(1, sections, greet_section, 0)
    pl.semaphore_wait(barrier, seq - 1 + sections - 1)

    def wo_copy(i):
        peer = (me + i) % seq
        return pltpu.make_async_remote_copy(
            src_ref=w_out.at[0, :, columns(peer)],
            dst_ref=out_weights.at[me],
            send_sem=wo_send.at[i],
            recv_sem=wo_recv.at[me],
            device_id=(section, peer),
            device_id_type=MESH,
        )

    def wo_start(i, carry):
        wo_copy(i).start()
        return carry

    lax.fori_loop(1, seq, wo_start, 0)

    def wo_wait(i, carry):
        peer = (me + i) % seq
        pltpu.make_async_remote_copy(
            src_ref=out_weights.at[peer],
            dst_ref=out_weights.at[peer],
            send_sem=wo_send.at[i],
            recv_sem=wo_recv.at[peer],
            device_id=(section, peer),
            device_id_type=MESH,
        ).wait_recv()
        return carry

    own_targets = ((1, 0, 0), (-1, 0, 0), (1, 1, 0), (-1, 1, 0), (0, 1, 0), (0, 0, 1))
    relayed = (
        ((1, 0, 0), 0, (-1, 0, 0)),
        ((-1, 0, 0), 1, (1, 0, 0)),
        ((1, 1, 0), 0, (-1, 0, 0)),
        ((-1, 1, 0), 1, (1, 0, 0)),
    )
    handed = ((1, 0, 0), (-1, 0, 0), (0, 1, 0), (1, 1, 0), (-1, 1, 0), (2, 0, 0), (2, 1, 0))

    class Gather:
        def __init__(self, buf, recv, send):
            self.buf, self.recv, self.send = buf, recv, send

        def copy(self, m, index):
            if index < 6:
                j, part, target = me, None, own_targets[index]
            elif index < 10:
                where, part, target = relayed[index - 6]
                j = at(*where)
            else:
                j, part, target = at(*handed[index - 10]), None, (0, 0, 1)
            ref = self.buf.at[m, j]
            if part is not None:
                ref = self.buf.at[m, j, pl.ds(part * half, half)]
            return pltpu.make_async_remote_copy(
                src_ref=ref,
                dst_ref=ref,
                send_sem=self.send.at[m, index],
                recv_sem=self.recv.at[m, 2 * j + (part or 0)],
                device_id=(section, at(*target)),
                device_id_type=MESH,
            )

        def begin(self, m):
            for index in range(6):
                self.copy(m, index).start()

        def arrived(self, m, j, part=None):
            ref = self.buf.at[m, j]
            if part is not None:
                ref = self.buf.at[m, j, pl.ds(part * half, half)]
            pltpu.make_async_remote_copy(
                src_ref=ref,
                dst_ref=ref,
                send_sem=self.send.at[m, 0],
                recv_sem=self.recv.at[m, 2 * j + (part or 0)],
                device_id=(section, at(0, 0, 1)),
                device_id_type=MESH,
            ).wait_recv()

        def entered(self, m):
            self.arrived(m, me)

        def process(self, m, use):
            def chip(dx, dy):
                self.arrived(m, at(dx, dy, 1))
                use(m, at(dx, dy, 0) // 2)

            self.arrived(m, at(1, 0, 0))
            self.copy(m, 6).start()
            self.copy(m, 10).start()
            self.arrived(m, at(-1, 0, 0))
            self.copy(m, 7).start()
            self.copy(m, 11).start()
            chip(0, 0)
            self.arrived(m, at(0, 1, 0))
            self.copy(m, 12).start()
            self.arrived(m, at(1, 1, 0))
            self.copy(m, 8).start()
            self.copy(m, 13).start()
            self.arrived(m, at(-1, 1, 0))
            self.copy(m, 9).start()
            self.copy(m, 14).start()
            chip(1, 0)
            chip(-1, 0)
            chip(0, 1)
            self.arrived(m, at(2, 0, 0), 0)
            self.arrived(m, at(2, 0, 0), 1)
            self.copy(m, 15).start()
            chip(1, 1)
            chip(-1, 1)
            self.arrived(m, at(2, 1, 0), 0)
            self.arrived(m, at(2, 1, 0), 1)
            self.copy(m, 16).start()
            chip(2, 0)
            chip(2, 1)

        def drain(self, m):
            for index in range(17):
                self.copy(m, index).wait_send()

    x_gather = Gather(x_buf, x_recv, x_send)
    mix_gather = Gather(mix_buf, mix_recv, mix_send)
    mem_gather = Gather(mem_buf, mem_recv, mem_send)
    out_gather = Gather(out_buf, out_recv, out_send)

    def clear():
        acc[...] = jnp.zeros_like(acc)
        squares[...] = jnp.zeros_like(squares)

    def project_block(buf, gains, first, stop, m, j):
        rows = buf[m, j].astype(F32)
        square = rows * rows
        squares[...] += square[:, : width // 2] + square[:, width // 2 :]
        scaled = (rows * gains[:, columns(j)]).astype(BF16)
        acc[:, first:stop] += jnp.dot(
            scaled, weights[columns(j), first:stop], preferred_element_type=F32
        )

    def projecting(buf, gains, first, stop):
        def use(m, q):
            project_block(buf, gains, first, stop, m, 2 * q)
            project_block(buf, gains, first, stop, m, 2 * q + 1)

        return use

    def local_project(m, gains, first, stop):
        clear()
        pltpu.make_async_copy(x_buf.at[m], x_buf.at[m], x_load.at[m]).wait()

        def one(j, carry):
            project_block(x_buf, gains, first, stop, m, j)
            return carry

        lax.fori_loop(0, blocks, one, 0)

    def gathered_project(gather, m, gains, first, stop):
        clear()
        gather.entered(m)
        gather.begin(m)
        gather.process(m, projecting(gather.buf, gains, first, stop))

    def row_factor():
        return lax.rsqrt(jnp.sum(squares[...], axis=1, keepdims=True) * (1.0 / features) + EPS)

    def unit(projected):
        square = projected * projected
        upper = square.astype(BF16)
        lower = (square - upper.astype(F32)).astype(BF16)
        row = lax.broadcasted_iota(jnp.int32, (width, width), 0) // head_size
        column = lax.broadcasted_iota(jnp.int32, (width, width), 1) // head_size
        spread = jnp.where(row == column, 1.0 / head_size, 0.0).astype(BF16)
        mean = jnp.dot(upper, spread, preferred_element_type=F32) + jnp.dot(
            lower, spread, preferred_element_type=F32
        )
        return (projected * lax.rsqrt(mean + EPS)).astype(BF16)

    def keep_query(m):
        q_unit[m] = unit(acc[:, :width] * row_factor())

    def keep_memory(m):
        factor = row_factor()
        k_unit[m] = unit(acc[:, width : 2 * width] * factor)
        v_rows[m] = (acc[:, 2 * width :] * factor).astype(BF16)

    def attend(m):
        queries = q_unit[m].astype(F32)
        keys = k_unit[m]
        values = v_rows[m]
        lane_head = lax.broadcasted_iota(jnp.int32, (length, width), 1) // head_size
        stacked = jnp.concatenate(
            [jnp.where(lane_head == h, queries, 0.0).astype(BF16) for h in range(heads)], axis=0
        )
        scores = lax.dot_general(
            stacked, keys, (((1,), (1,)), ((), ())), preferred_element_type=F32
        )
        mixture = jnp.zeros((length, width), F32)
        for h in range(heads):
            factor = sharpness[0, h] * (1.0 / head_size**0.5)
            grown = jnp.exp(scores[h * length : (h + 1) * length] * factor)
            total = jnp.sum(grown, axis=1, keepdims=True)
            share = (grown * (1.0 / total)).astype(BF16)
            mixed = jnp.dot(share, values, preferred_element_type=F32)
            mixture = jnp.where(lane_head == h, mixed, mixture)
        mix_buf[m, me] = mixture.astype(BF16)
        mix_gather.begin(m)

    full = 3 * width
    for load in loads:
        load.wait()

    def early(m, carry):
        @pl.when(section == encoders)
        def _():
            local_project(m, gain, 0, width)
            keep_query(m)

        @pl.when(section > encoders)
        def _():
            gathered_project(mem_gather, m, last_gain, width, full)
            keep_memory(m)

        return carry

    lax.fori_loop(0, batches, early, 0)

    def main(m, carry):
        @pl.when(section == 0)
        def _():
            local_project(m, gain, 0, full)

        @pl.when((section > 0) & (section < encoders))
        def _():
            gathered_project(x_gather, m, gain, 0, full)

        @pl.when(section < encoders)
        def _():
            keep_query(m)
            keep_memory(m)

        @pl.when(section == encoders)
        def _():
            gathered_project(mem_gather, m, last_gain, width, full)
            keep_memory(m)

        @pl.when(section > encoders)
        def _():
            gathered_project(x_gather, m, gain, 0, width)
            keep_query(m)

        attend(m)
        return carry

    lax.fori_loop(0, batches, main, 0)

    own_wo.wait()
    lax.fori_loop(1, seq, wo_wait, 0)

    def onward(m, target):
        return pltpu.make_async_remote_copy(
            src_ref=out_buf.at[m, me],
            dst_ref=x_buf.at[m, me],
            send_sem=next_send.at[m, 0],
            recv_sem=x_recv.at[m, 2 * me],
            device_id=(target, me),
            device_id_type=MESH,
        )

    def to_memory(m, i):
        return pltpu.make_async_remote_copy(
            src_ref=out_buf.at[m, me],
            dst_ref=mem_buf.at[m, me],
            send_sem=next_send.at[m, i],
            recv_sem=mem_recv.at[m, 2 * me],
            device_id=(encoders + i, me),
            device_id_type=MESH,
        )

    def project_out(m, q):
        for i in range(2):
            j = 2 * q + i
            out_acc[...] += jnp.dot(mix_buf[m, j], out_weights[j], preferred_element_type=F32)

    def finish(m, carry):
        out_acc[...] = x_buf[m, me].astype(F32)
        mix_gather.process(m, project_out)
        out_buf[m, me] = out_acc[...].astype(BF16)

        @pl.when((section < sections - 1) & (section != encoders - 1))
        def _():
            onward(m, section + 1).start()

        @pl.when(section == encoders - 1)
        def _():
            for i in range(sections - encoders):
                to_memory(m, i).start()

        return carry

    lax.fori_loop(0, batches, finish, 0)

    def store(m, q):
        for i in range(2):
            j = 2 * q + i
            pltpu.make_async_copy(
                out_buf.at[m, j], result.at[0, m, :, columns(j)], store_sem.at[m]
            ).start()

    def spread_begin(m, carry):
        out_gather.begin(m)
        return carry

    def spread(m, carry):
        out_gather.process(m, store)
        return carry

    lax.fori_loop(0, batches, spread_begin, 0)
    lax.fori_loop(0, batches, spread, 0)

    def drain(m, carry):
        mix_gather.drain(m)
        out_gather.drain(m)

        @pl.when((section > 0) & (section != encoders))
        def _():
            x_gather.drain(m)

        @pl.when(section >= encoders)
        def _():
            mem_gather.drain(m)

        @pl.when((section < sections - 1) & (section != encoders - 1))
        def _():
            onward(m, section + 1).wait_send()

        @pl.when(section == encoders - 1)
        def _():
            for i in range(sections - encoders):
                to_memory(m, i).wait_send()

        pltpu.make_async_copy(out_buf.at[m], out_buf.at[m], store_sem.at[m]).wait()
        return carry

    lax.fori_loop(0, batches, drain, 0)

    def wo_drain(i, carry):
        wo_copy(i).wait_send()
        return carry

    lax.fori_loop(1, seq, wo_drain, 0)


def solution(mesh):
    sections, seq = mesh.shape["section"], mesh.shape["seq"]

    def shards(inbound, decoder, w_query, w_key, w_value, w_out, gain, sharpness, last_gain):
        batches, length, features = inbound.shape
        width = features // seq
        blocks = pltpu.VMEM((batches, seq, length, width), BF16)
        small = pltpu.VMEM((batches, length, width), BF16)
        recv = pltpu.SemaphoreType.DMA((batches, 2 * seq))
        send = pltpu.SemaphoreType.DMA((batches, 17))
        anywhere = pl.BlockSpec(memory_space=pl.ANY)
        vmem = pl.BlockSpec(memory_space=pltpu.VMEM)
        return pl.pallas_call(
            kernel,
            out_shape=jax.ShapeDtypeStruct((1, batches, length, features), BF16),
            in_specs=[anywhere] * 6 + [vmem, pl.BlockSpec(memory_space=pltpu.SMEM), vmem],
            out_specs=anywhere,
            scratch_shapes=[
                pltpu.VMEM((features, 3 * width), BF16),
                pltpu.VMEM((seq, width, width), BF16),
                blocks,
                blocks,
                blocks,
                blocks,
                small,
                small,
                small,
                pltpu.VMEM((length, 3 * width), F32),
                pltpu.VMEM((length, width // 2), F32),
                pltpu.VMEM((length, width), F32),
                recv,
                recv,
                recv,
                recv,
                send,
                send,
                send,
                send,
                pltpu.SemaphoreType.DMA((batches, sections)),
                pltpu.SemaphoreType.DMA((seq,)),
                pltpu.SemaphoreType.DMA((seq,)),
                pltpu.SemaphoreType.DMA((4,)),
                pltpu.SemaphoreType.DMA((batches,)),
                pltpu.SemaphoreType.DMA((batches,)),
            ],
            compiler_params=pltpu.CompilerParams(
                collective_id=0, has_side_effects=True, vmem_limit_bytes=60 * 1024 * 1024
            ),
            name="cascade",
        )(
            inbound,
            decoder,
            w_query,
            w_key,
            w_value,
            w_out,
            gain,
            sharpness,
            last_gain.reshape(1, features),
        )

    return jax.shard_map(
        shards,
        mesh=mesh,
        in_specs=(
            P(),
            P(),
            P("section", None, "seq"),
            P("section", None, "seq"),
            P("section", None, "seq"),
            P("section", "seq", None),
            P("section", None),
            P("section", "seq"),
            P(),
        ),
        out_specs=P("section", None, None, None),
        check_vma=False,
    )
```

```python
import functools

import jax
import jax.numpy as jnp
from jax import lax
from jax.experimental import pallas as pl
from jax.experimental.pallas import tpu as pltpu
from jax.sharding import PartitionSpec as P

MESH = pl.DeviceIdType.MESH
EPS = 1e-06
F32 = jnp.float32
BF16 = jnp.bfloat16

RING = 4
CHIPS = 2 * RING
OTHERS = ((2, 1), (1, 1), (-1, 1), (2, 0), (0, 1), (1, 0), (-1, 0))
PER = 1

QUERY, KEY, VALUE = 0, 1, 2
PLANE = {QUERY: 0, KEY: 2, VALUE: 3}
SQUARES = 1


def kernel(
    inbound,
    decoder,
    w_query,
    w_key,
    w_value,
    w_out,
    gain,
    sharpness,
    last_gain,
    result,
    weights,
    out_weights,
    x_buf,
    mem_buf,
    mix_buf,
    part_buf,
    sum_buf,
    out_buf,
    swap_out,
    swap_in,
    own_acc,
    q_unit,
    k_unit,
    v_rows,
    x_recv,
    mem_recv,
    sum_recv,
    out_recv,
    x_send,
    mem_send,
    sum_send,
    out_send,
    next_send,
    swap_recv,
    swap_send,
    mix_recv,
    mix_send,
    load_sem,
    x_load,
    store_sem,
):
    sections = lax.axis_size("section")
    seq = lax.axis_size("seq")
    encoders = 3 * sections // 8
    section = lax.axis_index("section")
    me = lax.axis_index("seq")
    chunks, _, rows, width = x_buf.shape
    features = seq * width
    length = rows * PER
    heads = sharpness.shape[1]
    head_size = width // heads
    x_pos, y_pos, core = me // 4, (me // 2) % 2, me % 2
    here = me // 2
    partner = 2 * here + 1 - core

    def chip(dx, dy):
        return ((x_pos + dx) % RING) * 2 + (y_pos + dy) % 2

    def columns(j):
        return pl.ds(pl.multiple_of(j * width, width), width)

    def token_rows(ch):
        return pl.ds(pl.multiple_of((ch % PER) * rows, rows), rows)

    def remote(src, dst, send_sem, recv_sem, target):
        return pltpu.make_async_remote_copy(
            src_ref=src,
            dst_ref=dst,
            send_sem=send_sem,
            recv_sem=recv_sem,
            device_id=(section, target),
            device_id_type=MESH,
        )

    def landed(ref, recv_sem):
        remote(ref, ref, mix_send.at[0], recv_sem, partner).wait_recv()

    def load_x(source):
        def one(i, carry):
            ch, q = i // CHIPS, i % CHIPS
            pltpu.make_async_copy(
                source.at[ch // PER, token_rows(ch), columns(2 * q + core)],
                x_buf.at[ch, q],
                x_load.at[0],
            ).start()
            return carry

        lax.fori_loop(0, chunks * CHIPS, one, 0)

    pl.when(section == 0)(lambda: load_x(inbound))
    pl.when(section == encoders)(lambda: load_x(decoder))
    projections = (w_query, w_key, w_value)

    def load_own(q, carry):
        for i, w_ref in enumerate(projections):
            pltpu.make_async_copy(
                w_ref.at[0, columns(2 * q + core)], weights.at[i, q], load_sem.at[0]
            ).start()
        return carry

    def load_own_out(q, carry):
        pltpu.make_async_copy(
            w_out.at[0, :, columns(2 * q + core)], out_weights.at[core, q], load_sem.at[1]
        ).start()
        return carry

    lax.fori_loop(0, CHIPS, load_own, 0)
    lax.fori_loop(0, CHIPS, load_own_out, 0)

    barrier = pltpu.get_barrier_semaphore()

    def greet(target_section, target):
        pl.semaphore_signal(
            barrier, inc=1, device_id=(target_section, target), device_id_type=MESH
        )

    greet(section, partner)
    for other in OTHERS:
        greet(section, 2 * chip(*other) + core)
    lax.fori_loop(1, sections, lambda i, c: (greet((section + i) % sections, me), c)[1], 0)
    pl.semaphore_wait(barrier, CHIPS + sections - 1)

    def give(q, carry):
        for i, w_ref in enumerate(projections):
            remote(
                w_ref.at[0, columns(2 * q + 1 - core)],
                weights.at[3 + i, q],
                load_sem.at[2],
                load_sem.at[3],
                partner,
            ).start()
        return carry

    def give_out(q, carry):
        remote(
            w_out.at[0, :, columns(2 * q + 1 - core)],
            out_weights.at[core, q],
            load_sem.at[4],
            load_sem.at[5],
            partner,
        ).start()
        return carry

    lax.fori_loop(0, CHIPS, give, 0)
    lax.fori_loop(0, CHIPS, give_out, 0)

    def spread(buf, recv, send, ch):
        return [
            remote(
                buf.at[ch, here],
                buf.at[ch, here],
                send.at[ch, i],
                recv.at[ch, here],
                2 * chip(*other) + core,
            )
            for i, other in enumerate(OTHERS)
        ]

    def enter(buf, recv, send, ch):
        landed(buf.at[ch, here], recv.at[ch, here])
        for copy in spread(buf, recv, send, ch):
            copy.start()

    def swap(kind, ch, first, stop):
        return remote(
            swap_out.at[kind, ch, pl.ds(first, stop - first)],
            swap_in.at[kind, ch, pl.ds(first, stop - first)],
            swap_send.at[kind, ch],
            swap_recv.at[kind, ch],
            partner,
        )

    def project(buf, recv, ch, gains, wanted, kind, gathered):
        order = ((0, 0),) + OTHERS
        for first in range(0, CHIPS, 2):
            parts = []
            for other in order[first : first + 2]:
                q = chip(*other)
                if other != (0, 0):
                    pl.when(gathered)(lambda: landed(buf.at[ch, q], recv.at[ch, q]))
                block = buf[ch, q].astype(F32)
                scaled = (block * gains[:, columns(2 * q + core)]).astype(BF16)
                parts.append((q, block * block, scaled))
            square = parts[0][1] + parts[1][1]
            swap_out[kind, ch, SQUARES] = (
                square if first == 0 else swap_out[kind, ch, SQUARES] + square
            )
            for p in wanted:
                for side in range(2):
                    product = sum(
                        jnp.dot(scaled, weights[3 * side + p, q], preferred_element_type=F32)
                        for q, _, scaled in parts
                    )
                    if side == 0:
                        own_acc[p] = product if first == 0 else own_acc[p] + product
                    else:
                        at = PLANE[p]
                        swap_out[kind, ch, at] = (
                            product if first == 0 else swap_out[kind, ch, at] + product
                        )
        first = min(SQUARES, min(PLANE[p] for p in wanted))
        stop = 1 + max(SQUARES, max(PLANE[p] for p in wanted))
        exchange = swap(kind, ch, first, stop)
        exchange.start()
        exchange.wait_recv()
        squares = swap_out[kind, ch, SQUARES] + swap_in[kind, ch, SQUARES]
        factor = lax.rsqrt(jnp.sum(squares, axis=1, keepdims=True) * (1.0 / features) + EPS)
        for p in wanted:
            total = (own_acc[p] + swap_in[kind, ch, PLANE[p]]) * factor
            if p == QUERY:
                q_unit[ch] = unit(total)
            elif p == KEY:
                k_unit[ch // PER, token_rows(ch)] = unit(total)
            else:
                v_rows[ch // PER, token_rows(ch)] = total.astype(BF16)

    def unit(projected):
        square = projected * projected
        upper = square.astype(BF16)
        lower = (square - upper.astype(F32)).astype(BF16)
        row = lax.broadcasted_iota(jnp.int32, (width, width), 0) // head_size
        column = lax.broadcasted_iota(jnp.int32, (width, width), 1) // head_size
        same = jnp.where(row == column, 1.0 / head_size, 0.0).astype(BF16)
        mean = jnp.dot(upper, same, preferred_element_type=F32) + jnp.dot(
            lower, same, preferred_element_type=F32
        )
        return (projected * lax.rsqrt(mean + EPS)).astype(BF16)

    def mix_swap(ch):
        return remote(
            mix_buf.at[ch, core], mix_buf.at[ch, core], mix_send.at[ch], mix_recv.at[ch], partner
        )

    def partial(ch, i):
        q = chip(*OTHERS[i])
        return remote(
            part_buf.at[ch, q],
            sum_buf.at[ch, here],
            sum_send.at[ch, i],
            sum_recv.at[ch, here],
            2 * q + core,
        )

    def attend(ch):
        queries = q_unit[ch].astype(F32)
        keys = k_unit[ch // PER]
        values = v_rows[ch // PER]
        lane_head = lax.broadcasted_iota(jnp.int32, (rows, width), 1) // head_size
        stacked = jnp.concatenate(
            [jnp.where(lane_head == h, queries, 0.0).astype(BF16) for h in range(heads)], axis=0
        )
        scores = lax.dot_general(
            stacked, keys, (((1,), (1,)), ((), ())), preferred_element_type=F32
        )
        mixture = jnp.zeros((rows, width), F32)
        for h in range(heads):
            factor = sharpness[0, h] * (1.0 / head_size**0.5)
            grown = jnp.exp(scores[h * rows : (h + 1) * rows] * factor)
            total = jnp.sum(grown, axis=1, keepdims=True)
            share = (grown * (1.0 / total)).astype(BF16)
            mixed = jnp.dot(share, values, preferred_element_type=F32)
            mixture = jnp.where(lane_head == h, mixed, mixture)
        mix_buf[ch, core] = mixture.astype(BF16)
        mix_swap(ch).start()

    def project_out(ch):
        landed(mix_buf.at[ch, 1 - core], mix_recv.at[ch])
        mixture = [mix_buf[ch, 0], mix_buf[ch, 1]]

        def product(q):
            return sum(
                jnp.dot(mixture[i], out_weights[i, q], preferred_element_type=F32)
                for i in range(2)
            )

        for i, other in enumerate(OTHERS):
            q = chip(*other)
            part_buf[ch, q] = product(q).astype(BF16)
            partial(ch, i).start()
        part_buf[ch, here] = product(here).astype(BF16)

    def onward(ch):
        return pltpu.make_async_remote_copy(
            src_ref=out_buf.at[ch, me],
            dst_ref=x_buf.at[ch, here],
            send_sem=next_send.at[ch, 0],
            recv_sem=x_recv.at[ch, here],
            device_id=(section + 1, me),
            device_id_type=MESH,
        )

    def to_memory(ch, i):
        return pltpu.make_async_remote_copy(
            src_ref=out_buf.at[ch, me],
            dst_ref=mem_buf.at[ch, here],
            send_sem=next_send.at[ch, i],
            recv_sem=mem_recv.at[ch, here],
            device_id=(encoders + i, me),
            device_id_type=MESH,
        )

    def share(ch, i):
        target = 2 * chip(*OTHERS[i]) + core if i < CHIPS - 1 else partner
        return remote(
            out_buf.at[ch, me], out_buf.at[ch, me], out_send.at[ch, i], out_recv.at[ch, me], target
        )

    def hand(ch, i):
        j = 2 * chip(*OTHERS[i]) + core
        return remote(
            out_buf.at[ch, j],
            out_buf.at[ch, j],
            out_send.at[ch, CHIPS + i],
            out_recv.at[ch, j],
            partner,
        )

    def share_begin(ch, carry=0):
        share(ch, CHIPS - 1).start()
        for i in range(CHIPS - 1):
            share(ch, i).start()
        return carry

    def store(ch, j):
        pltpu.make_async_copy(
            out_buf.at[ch, j],
            result.at[0, ch // PER, token_rows(ch), columns(j)],
            store_sem.at[0],
        ).start()

    def share_end(ch, carry):
        store(ch, me)
        for i, other in enumerate(OTHERS):
            j = 2 * chip(*other) + core
            landed(out_buf.at[ch, j], out_recv.at[ch, j])
            hand(ch, i).start()
            store(ch, j)
        for other in ((0, 0),) + OTHERS:
            j = 2 * chip(*other) + 1 - core
            landed(out_buf.at[ch, j], out_recv.at[ch, j])
            store(ch, j)
        return carry

    def reduce(ch):
        total = x_buf[ch, here].astype(F32) + part_buf[ch, here].astype(F32)
        for other in OTHERS:
            q = chip(*other)
            landed(sum_buf.at[ch, q], sum_recv.at[ch, q])
            total = total + sum_buf[ch, q].astype(F32)
        out_buf[ch, me] = total.astype(BF16)

        @pl.when((section < sections - 1) & (section != encoders - 1))
        def _():
            onward(ch).start()

        @pl.when(section == encoders - 1)
        def _():
            for i in range(sections - encoders):
                to_memory(ch, i).start()

        @pl.when(section == sections - 1)
        def _():
            share_begin(ch)

    pltpu.make_async_copy(weights.at[:3], weights.at[:3], load_sem.at[0]).wait()
    remote(weights.at[3:], weights.at[3:], load_sem.at[2], load_sem.at[3], partner).wait()

    @pl.when((section == 0) | (section == encoders))
    def _():
        pltpu.make_async_copy(x_buf, x_buf, x_load.at[0]).wait()

    ahead_x = (x_buf, x_recv)
    ahead_mem = (mem_buf, mem_recv)

    def early_enter(ch, carry):
        enter(mem_buf, mem_recv, mem_send, ch)
        return carry

    def early(ch, carry):
        @pl.when(section == encoders)
        def _():
            project(*ahead_x, ch, gain, (QUERY,), 0, False)

        @pl.when(section > encoders)
        def _():
            project(*ahead_mem, ch, last_gain, (KEY, VALUE), 1, True)

        return carry

    @pl.when(section > encoders)
    def _():
        lax.fori_loop(0, chunks, early_enter, 0)

    @pl.when(section >= encoders)
    def _():
        lax.fori_loop(0, chunks, early, 0)

    pltpu.make_async_copy(out_weights.at[0], out_weights.at[0], load_sem.at[1]).wait()
    remote(out_weights.at[0], out_weights.at[0], load_sem.at[4], load_sem.at[5], partner).wait()

    def begin(ch):
        @pl.when((section > 0) & (section != encoders))
        def _():
            enter(x_buf, x_recv, x_send, ch)

        @pl.when(section == encoders)
        def _():
            enter(mem_buf, mem_recv, mem_send, ch)

    def advance(ch):
        @pl.when(section < encoders)
        def _():
            project(*ahead_x, ch, gain, (QUERY, KEY, VALUE), 0, section > 0)

        @pl.when(section == encoders)
        def _():
            project(*ahead_mem, ch, last_gain, (KEY, VALUE), 1, True)

        @pl.when(section > encoders)
        def _():
            project(*ahead_x, ch, gain, (QUERY,), 0, True)

        if PER == 1:
            attend(ch)
            project_out(ch)
        else:

            @pl.when(section > encoders)
            def _():
                attend(ch)
                project_out(ch)

            @pl.when((section <= encoders) & (ch % PER == PER - 1))
            def _():
                for i in range(PER):
                    attend(ch - PER + 1 + i)
                for i in range(PER):
                    project_out(ch - PER + 1 + i)

    begin(0)

    def step(t, carry):
        pl.when(t + 1 < chunks)(lambda: begin(t + 1))
        pl.when(t < chunks)(lambda: advance(t))
        pl.when(t >= LAG)(lambda: reduce(t - LAG))
        return carry

    LAG = PER
    lax.fori_loop(0, chunks + LAG, step, 0)

    @pl.when(section < sections - 1)
    def _():
        lax.fori_loop(0, chunks, share_begin, 0)

    lax.fori_loop(0, chunks, share_end, 0)

    def drain(ch, carry):
        mix_swap(ch).wait_send()
        for i in range(CHIPS - 1):
            partial(ch, i).wait_send()
            share(ch, i).wait_send()
            hand(ch, i).wait_send()
        share(ch, CHIPS - 1).wait_send()

        @pl.when(section < encoders)
        def _():
            swap(0, ch, 0, 4).wait_send()

        @pl.when(section >= encoders)
        def _():
            swap(0, ch, 0, 2).wait_send()
            swap(1, ch, 1, 4).wait_send()
            for copy in spread(mem_buf, mem_recv, mem_send, ch):
                copy.wait_send()

        @pl.when((section > 0) & (section != encoders))
        def _():
            for copy in spread(x_buf, x_recv, x_send, ch):
                copy.wait_send()

        @pl.when((section < sections - 1) & (section != encoders - 1))
        def _():
            onward(ch).wait_send()

        @pl.when(section == encoders - 1)
        def _():
            for i in range(sections - encoders):
                to_memory(ch, i).wait_send()

        return carry

    lax.fori_loop(0, chunks, drain, 0)
    pltpu.make_async_copy(out_buf, out_buf, store_sem.at[0]).wait()


def solution(mesh):
    sections, seq = mesh.shape["section"], mesh.shape["seq"]

    def shards(inbound, decoder, w_query, w_key, w_value, w_out, gain, sharpness, last_gain):
        batches, length, features = inbound.shape
        width = features // seq
        chunks, rows = batches * PER, length // PER
        dma = pltpu.SemaphoreType.DMA
        blocks = pltpu.VMEM((chunks, CHIPS, rows, width), BF16)
        swapped = pltpu.VMEM((2, chunks, 4, rows, width), F32)
        anywhere = pl.BlockSpec(memory_space=pl.ANY)
        vmem = pl.BlockSpec(memory_space=pltpu.VMEM)
        return pl.pallas_call(
            kernel,
            out_shape=jax.ShapeDtypeStruct((1, batches, length, features), BF16),
            in_specs=[anywhere] * 6 + [vmem, pl.BlockSpec(memory_space=pltpu.SMEM), vmem],
            out_specs=anywhere,
            scratch_shapes=[
                pltpu.VMEM((6, CHIPS, width, width), BF16),
                pltpu.VMEM((2, CHIPS, width, width), BF16),
                blocks,
                blocks,
                pltpu.VMEM((chunks, 2, rows, width), BF16),
                blocks,
                blocks,
                pltpu.VMEM((chunks, seq, rows, width), BF16),
                swapped,
                swapped,
                pltpu.VMEM((3, rows, width), F32),
                pltpu.VMEM((chunks, rows, width), BF16),
                pltpu.VMEM((batches, length, width), BF16),
                pltpu.VMEM((batches, length, width), BF16),
                dma((chunks, CHIPS)),
                dma((chunks, CHIPS)),
                dma((chunks, CHIPS)),
                dma((chunks, seq)),
                dma((chunks, CHIPS - 1)),
                dma((chunks, CHIPS - 1)),
                dma((chunks, CHIPS - 1)),
                dma((chunks, seq)),
                dma((chunks, sections)),
                dma((2, chunks)),
                dma((2, chunks)),
                dma((chunks,)),
                dma((chunks,)),
                dma((6,)),
                dma((1,)),
                dma((1,)),
            ],
            compiler_params=pltpu.CompilerParams(
                collective_id=0, has_side_effects=True, vmem_limit_bytes=60 * 1024 * 1024
            ),
            name="cascade",
        )(
            inbound,
            decoder,
            w_query,
            w_key,
            w_value,
            w_out,
            gain,
            sharpness,
            last_gain.reshape(1, features),
        )

    return jax.shard_map(
        shards,
        mesh=mesh,
        in_specs=(
            P(),
            P(),
            P("section", None, "seq"),
            P("section", None, "seq"),
            P("section", None, "seq"),
            P("section", "seq", None),
            P("section", None),
            P("section", "seq"),
            P(),
        ),
        out_specs=P("section", None, None, None),
        check_vma=False,
    )
```

```python
import jax
import jax.numpy as jnp
from jax import lax
from jax.experimental import pallas as pl
from jax.experimental.pallas import tpu as pltpu
from jax.sharding import PartitionSpec as P

MESH = pl.DeviceIdType.MESH
EPS = 1e-06
F32 = jnp.float32
BF16 = jnp.bfloat16

RING = 4
CHIPS = 2 * RING
CORES = 2
OTHERS = ((2, 1), (1, 1), (-1, 1), (2, 0), (0, 1), (1, 0), (-1, 0))
SUB = 8

QUERY, KEY, VALUE = 0, 1, 2


def kernel(
    inbound,
    decoder,
    w_query,
    w_key,
    w_value,
    w_out,
    gain,
    sharpness,
    last_gain,
    result,
    weights,
    out_weights,
    all_x,
    x_buf,
    mem_buf,
    mix_buf,
    mix_out,
    part_buf,
    sum_buf,
    own_out,
    acc,
    squares,
    q_unit,
    k_unit,
    v_rows,
    sharp,
    x_recv,
    mem_recv,
    sum_recv,
    out_recv,
    x_send,
    mem_send,
    sum_send,
    out_send,
    next_send,
    local_sem,
    pair_recv,
    pair_send,
    gate,
):
    sections = lax.axis_size("section")
    encoders = 3 * sections // 8
    section = lax.axis_index("section")
    me = lax.axis_index("seq")
    _, length, wide = x_buf.shape
    width = wide // CORES
    features = CHIPS * wide
    part = length // SUB
    heads = sharpness.shape[1]
    head_size = width // heads
    x_pos, y_pos, core = me // 4, (me // 2) % 2, me % 2
    here = me // 2
    partner = 2 * here + 1 - core

    def chip(dx, dy):
        return ((x_pos + dx) % RING) * 2 + (y_pos + dy) % 2

    def span(q):
        return pl.ds(pl.multiple_of(q * wide, wide), wide)

    def piece(u):
        return pl.ds(u * part, part)

    def cell(m, u, q):
        return result.at[0, m, piece(u), span(q)]

    def remote(src, dst, send_sem, recv_sem, target):
        return pltpu.make_async_remote_copy(
            src_ref=src,
            dst_ref=dst,
            send_sem=send_sem,
            recv_sem=recv_sem,
            device_id=(section, target),
            device_id_type=MESH,
        )

    def landed(ref, recv_sem):
        remote(ref, ref, pair_send.at[0], recv_sem, partner).wait_recv()

    barrier = pltpu.get_barrier_semaphore()

    def greet(target_section, target):
        pl.semaphore_signal(
            barrier, inc=1, device_id=(target_section, target), device_id_type=MESH
        )

    greet(section, partner)
    for other in OTHERS:
        greet(section, 2 * chip(*other) + core)
    lax.fori_loop(1, sections, lambda i, c: (greet((section + i) % sections, me), c)[1], 0)

    @pl.when(section == 0)
    def _():
        def one(i, carry):
            m, q = i // CHIPS, i % CHIPS
            pltpu.make_async_copy(
                inbound.at[m, :, span(q)], all_x.at[m, q], local_sem.at[0]
            ).start()
            return carry

        lax.fori_loop(0, CORES * CHIPS, one, 0)
        pltpu.make_async_copy(
            inbound.at[core, :, span(here)], x_buf.at[here], local_sem.at[1]
        ).start()

    @pl.when(section == encoders)
    def _():
        def one(q, carry):
            pltpu.make_async_copy(
                decoder.at[core, :, span(q)], x_buf.at[q], local_sem.at[1]
            ).start()
            return carry

        lax.fori_loop(0, CHIPS, one, 0)

    projections = (w_query, w_key, w_value)
    own_weights = [
        pltpu.make_async_copy(w.at[0], weights.at[p, core], local_sem.at[2 + p])
        for p, w in enumerate(projections)
    ]
    own_out_weights = pltpu.make_async_copy(w_out.at[0], out_weights.at[core], local_sem.at[5])
    for copy in own_weights:
        copy.start()
    own_out_weights.start()
    row = lax.broadcasted_iota(jnp.int32, sharp.shape[1:], 0)
    filled = jnp.zeros(sharp.shape[1:], F32)
    for h in range(heads):
        filled = jnp.where(row == h, sharpness[0, h] * (1.0 / head_size**0.5), filled)
    sharp[core] = filled

    give = [
        remote(w.at[0], weights.at[p, core], pair_send.at[p], pair_recv.at[p], partner)
        for p, w in enumerate(projections)
    ]
    give_out = remote(
        w_out.at[0], out_weights.at[core], pair_send.at[3], pair_recv.at[3], partner
    )
    give_sharp = remote(sharp.at[core], sharp.at[core], pair_send.at[4], pair_recv.at[4], partner)
    give_mix = remote(mix_out, mix_buf.at[core], pair_send.at[5], pair_recv.at[5], partner)

    def spread(buf, recv, send, u):
        ref = buf.at[here, piece(u)]
        return [
            remote(ref, ref, send.at[u, i], recv.at[u, here], 2 * chip(*other) + core)
            for i, other in enumerate(OTHERS)
        ]

    def arrive(buf, recv, u, q):
        landed(buf.at[q, piece(u)], recv.at[u, q])

    def enter(buf, recv, send, ahead=None):
        for u in range(SUB):
            arrive(buf, recv, u, here)
            if ahead is not None:
                pl.when(section < sections - 1)(lambda: ahead(buf.at[here], u).start())
            for copy in spread(buf, recv, send, u):
                copy.start()

    def fold(block):
        square = block * block
        return square[:, :width] + square[:, width:]

    def project(buf, recv, gains, wanted, gathered):
        for step, other in enumerate(((0, 0),) + OTHERS):
            q = chip(*other)
            if gathered and step > 0:
                for u in range(SUB):
                    arrive(buf, recv, u, q)
            block = buf[q].astype(F32)
            squares[...] = fold(block) if step == 0 else squares[...] + fold(block)
            scaled = (block * gains[:, span(q)]).astype(BF16)
            for p in wanted:
                for side in range(CORES):
                    product = jnp.dot(
                        scaled, weights[p, side, span(q)], preferred_element_type=F32
                    )
                    acc[p, side] = product if step == 0 else acc[p, side] + product
        factor = row_factor()
        for p in wanted:
            for side in range(CORES):
                keep(p, side, acc[p, side] * factor)

    def project_local(m):
        for q in range(CHIPS):
            block = all_x[m, q].astype(F32)
            squares[...] = fold(block) if q == 0 else squares[...] + fold(block)
            scaled = (block * gain[:, span(q)]).astype(BF16)
            for p in (QUERY, KEY, VALUE):
                product = jnp.dot(scaled, weights[p, core, span(q)], preferred_element_type=F32)
                acc[p, 0] = product if q == 0 else acc[p, 0] + product
        factor = row_factor()
        for p in (QUERY, KEY, VALUE):
            keep(p, core, acc[p, 0] * factor)

    def row_factor():
        return lax.rsqrt(
            jnp.sum(squares[...], axis=1, keepdims=True) * (1.0 / features) + EPS
        )

    def keep(p, side, total):
        if p == QUERY:
            q_unit[side] = unit(total)
        elif p == KEY:
            k_unit[side] = unit(total)
        else:
            v_rows[side] = total.astype(BF16)

    def unit(projected):
        square = projected * projected
        upper = square.astype(BF16)
        lower = (square - upper.astype(F32)).astype(BF16)
        row = lax.broadcasted_iota(jnp.int32, (width, width), 0) // head_size
        column = lax.broadcasted_iota(jnp.int32, (width, width), 1) // head_size
        same = jnp.where(row == column, 1.0 / head_size, 0.0).astype(BF16)
        mean = jnp.dot(upper, same, preferred_element_type=F32) + jnp.dot(
            lower, same, preferred_element_type=F32
        )
        return (projected * lax.rsqrt(mean + EPS)).astype(BF16)

    def attend(side):
        queries = q_unit[side].astype(F32)
        keys = k_unit[side]
        values = v_rows[side]
        lane_head = lax.broadcasted_iota(jnp.int32, (length, width), 1) // head_size
        stacked = jnp.concatenate(
            [jnp.where(lane_head == h, queries, 0.0).astype(BF16) for h in range(heads)], axis=0
        )
        scores = lax.dot_general(
            stacked, keys, (((1,), (1,)), ((), ())), preferred_element_type=F32
        )
        mixture = jnp.zeros((length, width), F32)
        for h in range(heads):
            grown = jnp.exp(scores[h * length : (h + 1) * length] * sharp[side, pl.ds(h, 1)])
            total = jnp.sum(grown, axis=1, keepdims=True)
            share = (grown * (1.0 / total)).astype(BF16)
            mixed = jnp.dot(share, values, preferred_element_type=F32)
            mixture = jnp.where(lane_head == h, mixed, mixture)
        return mixture.astype(BF16)

    def partial(u, i):
        q = chip(*OTHERS[i])
        return remote(
            part_buf.at[q, piece(u)],
            sum_buf.at[here, piece(u)],
            sum_send.at[u, i],
            sum_recv.at[u, here],
            2 * q + core,
        )

    def project_out():
        mixture = [mix_buf[side] for side in range(CORES)]

        def product(q):
            return sum(
                jnp.dot(mixture[side], out_weights[side, :, span(q)], preferred_element_type=F32)
                for side in range(CORES)
            )

        for i, other in enumerate(OTHERS):
            q = chip(*other)
            part_buf[q] = product(q).astype(BF16)
            partial(0, i).start()
        for u in range(1, SUB):
            for i in range(CHIPS - 1):
                partial(u, i).start()
        part_buf[here] = product(here).astype(BF16)

    def onward(u):
        return pltpu.make_async_remote_copy(
            src_ref=own_out.at[piece(u)],
            dst_ref=x_buf.at[here, piece(u)],
            send_sem=next_send.at[u, 0],
            recv_sem=x_recv.at[u, here],
            device_id=(section + 1, me),
            device_id_type=MESH,
        )

    def remember(source, u):
        return pltpu.make_async_remote_copy(
            src_ref=source.at[piece(u)],
            dst_ref=mem_buf.at[here, piece(u)],
            send_sem=next_send.at[u, 1],
            recv_sem=mem_recv.at[u, here],
            device_id=(section + 1, me),
            device_id_type=MESH,
        )

    def share(u, i):
        target = 2 * chip(*OTHERS[i]) + core if i < CHIPS - 1 else partner
        return remote(
            own_out.at[piece(u)],
            cell(core, u, here),
            out_send.at[u, i],
            out_recv.at[core, u, here],
            target,
        )

    def hand(u, i):
        q = chip(*OTHERS[i])
        ref = cell(core, u, q)
        return remote(ref, ref, out_send.at[u, CHIPS + i], out_recv.at[core, u, q], partner)

    def share_begin(u):
        for i in range(CHIPS - 1):
            share(u, i).start()

    def reduce():
        for u in range(SUB):
            at = piece(u)
            total = x_buf[here, at].astype(F32) + part_buf[here, at].astype(F32)
            for other in OTHERS:
                q = chip(*other)
                arrive(sum_buf, sum_recv, u, q)
                total = total + sum_buf[q, at].astype(F32)
            rounded = total.astype(BF16)
            own_out[at] = rounded

            @pl.when((section < sections - 1) & (section != encoders - 1))
            def _():
                onward(u).start()

            @pl.when(section == encoders - 1)
            def _():
                remember(own_out, u).start()

            @pl.when(section == sections - 1)
            def _():
                share(u, CHIPS - 1).start()
                share_begin(u)

            result[0, core, at, span(here)] = rounded

    @pl.when(section == 0)
    def _():
        pltpu.make_async_copy(all_x, all_x, local_sem.at[0]).wait()

    for copy in own_weights:
        copy.wait()

    def local_mixture(m):
        project_local(m)
        mixture = attend(core)

        @pl.when(core == m)
        def _():
            mix_buf[core] = mixture

        @pl.when(core != m)
        def _():
            mix_out[...] = mixture

    pl.when(section == 0)(lambda: local_mixture(0))

    pl.semaphore_wait(barrier, CHIPS + sections - 1)

    @pl.when((section == 0) & (core != 0))
    def _():
        give_mix.start()

    give_out.start()
    give_sharp.start()

    @pl.when(section > 0)
    def _():
        for copy in give:
            copy.start()

    own_out_weights.wait()

    @pl.when(section == 0)
    def _():
        pltpu.make_async_copy(
            inbound.at[core, :, span(here)], x_buf.at[here], local_sem.at[1]
        ).wait()
        give_out.wait_recv()

        @pl.when(core == 0)
        def _():
            landed(mix_buf.at[1 - core], pair_recv.at[5])
            project_out()

        local_mixture(1)

        @pl.when(core == 0)
        def _():
            reduce()
            pl.semaphore_wait(gate, 1)
            give_mix.start()

        @pl.when(core != 0)
        def _():
            landed(mix_buf.at[1 - core], pair_recv.at[5])
            project_out()
            reduce()

        give_sharp.wait_recv()

    @pl.when(section > 0)
    def _():
        give_sharp.wait_recv()
        for copy in give:
            copy.wait_recv()
        everything, context = (QUERY, KEY, VALUE), (KEY, VALUE)

        @pl.when(section == encoders)
        def _():
            pltpu.make_async_copy(x_buf, x_buf, local_sem.at[1]).wait()
            project(x_buf, x_recv, gain, (QUERY,), False)
            enter(mem_buf, mem_recv, mem_send, remember)
            project(mem_buf, mem_recv, last_gain, context, True)

        @pl.when(section > encoders)
        def _():
            enter(mem_buf, mem_recv, mem_send, remember)
            project(mem_buf, mem_recv, last_gain, context, True)
            enter(x_buf, x_recv, x_send)
            project(x_buf, x_recv, gain, (QUERY,), True)

        @pl.when(section < encoders)
        def _():
            enter(x_buf, x_recv, x_send)

            @pl.when((section == 1) & (core == 0))
            def _():
                pl.semaphore_signal(gate, inc=1, device_id=(0, me), device_id_type=MESH)

            project(x_buf, x_recv, gain, everything, True)

        for side in range(CORES):
            mix_buf[side] = attend(side)
        give_out.wait_recv()
        project_out()
        reduce()

    @pl.when(section < sections - 1)
    def _():
        for u in range(SUB):
            pl.when(section != encoders - 1)(lambda: onward(u).wait_send())
            pl.when(section == encoders - 1)(lambda: remember(own_out, u).wait_send())
        for u in range(SUB):
            share(u, CHIPS - 1).start()

    for u in range(SUB):
        landed(cell(1 - core, u, here), out_recv.at[1 - core, u, here])

    @pl.when(section < sections - 1)
    def _():
        for u in range(SUB):
            share_begin(u)

    for u in range(SUB):
        for i, other in enumerate(OTHERS):
            q = chip(*other)
            landed(cell(core, u, q), out_recv.at[core, u, q])
            hand(u, i).start()
    for u in range(SUB):
        for other in OTHERS:
            q = chip(*other)
            landed(cell(1 - core, u, q), out_recv.at[1 - core, u, q])

    give_out.wait_send()
    give_sharp.wait_send()
    pl.when(section == 0)(lambda: give_mix.wait_send())

    @pl.when(section > 0)
    def _():
        for copy in give:
            copy.wait_send()

    for u in range(SUB):
        for i in range(CHIPS - 1):
            partial(u, i).wait_send()
            hand(u, i).wait_send()
        for i in range(CHIPS):
            share(u, i).wait_send()

        @pl.when(section >= encoders)
        def _():
            for copy in spread(mem_buf, mem_recv, mem_send, u):
                copy.wait_send()

        @pl.when((section > 0) & (section != encoders))
        def _():
            for copy in spread(x_buf, x_recv, x_send, u):
                copy.wait_send()

        @pl.when((section >= encoders) & (section < sections - 1))
        def _():
            remember(own_out, u).wait_send()


def solution(mesh):
    sections, seq = mesh.shape["section"], mesh.shape["seq"]

    def shards(inbound, decoder, w_query, w_key, w_value, w_out, gain, sharpness, last_gain):
        batches, length, features = inbound.shape
        width = features // seq
        wide = CORES * width
        dma = pltpu.SemaphoreType.DMA
        blocks = pltpu.VMEM((CHIPS, length, wide), BF16)
        planes = pltpu.VMEM((CORES, length, width), BF16)
        outside = pl.BlockSpec(memory_space=pltpu.HBM)
        vmem = pl.BlockSpec(memory_space=pltpu.VMEM)
        return pl.pallas_call(
            kernel,
            out_shape=jax.ShapeDtypeStruct((1, batches, length, features), BF16),
            in_specs=[outside] * 6 + [vmem, pl.BlockSpec(memory_space=pltpu.SMEM), vmem],
            out_specs=vmem,
            scratch_shapes=[
                pltpu.VMEM((3, CORES, features, width), BF16),
                pltpu.VMEM((CORES, width, features), BF16),
                pltpu.VMEM((batches, CHIPS, length, wide), BF16),
                blocks,
                blocks,
                planes,
                pltpu.VMEM((length, width), BF16),
                blocks,
                blocks,
                pltpu.VMEM((length, wide), BF16),
                pltpu.VMEM((3, CORES, length, width), F32),
                pltpu.VMEM((length, width), F32),
                planes,
                planes,
                planes,
                pltpu.VMEM((CORES, 8, length), F32),
                dma((SUB, CHIPS)),
                dma((SUB, CHIPS)),
                dma((SUB, CHIPS)),
                dma((CORES, SUB, CHIPS)),
                dma((SUB, CHIPS - 1)),
                dma((SUB, CHIPS - 1)),
                dma((SUB, CHIPS - 1)),
                dma((SUB, 2 * CHIPS)),
                dma((SUB, 2)),
                dma((6,)),
                dma((6,)),
                dma((6,)),
                pltpu.SemaphoreType.REGULAR,
            ],
            compiler_params=pltpu.CompilerParams(
                collective_id=0, has_side_effects=True, vmem_limit_bytes=60 * 1024 * 1024
            ),
            name="cascade",
        )(
            inbound,
            decoder,
            w_query,
            w_key,
            w_value,
            w_out,
            gain,
            sharpness,
            last_gain.reshape(1, features),
        )

    return jax.shard_map(
        shards,
        mesh=mesh,
        in_specs=(
            P(),
            P(),
            P("section", None, "seq"),
            P("section", None, "seq"),
            P("section", None, "seq"),
            P("section", "seq", None),
            P("section", None),
            P("section", "seq"),
            P(),
        ),
        out_specs=P("section", None, None, None),
        check_vma=False,
    )
```

```python
import jax
import jax.numpy as jnp
from jax import lax
from jax.experimental import pallas as pl
from jax.experimental.pallas import tpu as pltpu
from jax.sharding import PartitionSpec as P

MESH = pl.DeviceIdType.MESH
EPS = 1e-06
F32 = jnp.float32
BF16 = jnp.bfloat16

RING = 4
CHIPS = 2 * RING
CORES = 2
OTHERS = ((2, 1), (1, 1), (-1, 1), (2, 0), (0, 1), (1, 0), (-1, 0))
SUB = 4

QUERY, KEY, VALUE = 0, 1, 2


def kernel(
    inbound,
    decoder,
    w_query,
    w_key,
    w_value,
    w_out,
    gain,
    sharpness,
    last_gain,
    result,
    weights,
    out_weights,
    all_x,
    x_buf,
    mem_buf,
    mix_buf,
    mix_out,
    part_buf,
    sum_buf,
    own_out,
    acc,
    squares,
    q_unit,
    k_unit,
    v_rows,
    sharp,
    x_recv,
    mem_recv,
    sum_recv,
    out_recv,
    x_send,
    mem_send,
    sum_send,
    out_send,
    next_send,
    local_sem,
    pair_recv,
    pair_send,
):
    sections = lax.axis_size("section")
    encoders = 3 * sections // 8
    section = lax.axis_index("section")
    me = lax.axis_index("seq")
    _, length, wide = x_buf.shape
    width = wide // CORES
    features = CHIPS * wide
    part = length // SUB
    heads = sharpness.shape[1]
    head_size = width // heads
    x_pos, y_pos, core = me // 4, (me // 2) % 2, me % 2
    here = me // 2
    partner = 2 * here + 1 - core

    def chip(dx, dy):
        return ((x_pos + dx) % RING) * 2 + (y_pos + dy) % 2

    def span(q):
        return pl.ds(pl.multiple_of(q * wide, wide), wide)

    def piece(u):
        return pl.ds(u * part, part)

    def cell(m, u, q):
        return result.at[0, m, piece(u), span(q)]

    def remote(src, dst, send_sem, recv_sem, target):
        return pltpu.make_async_remote_copy(
            src_ref=src,
            dst_ref=dst,
            send_sem=send_sem,
            recv_sem=recv_sem,
            device_id=(section, target),
            device_id_type=MESH,
        )

    def landed(ref, recv_sem):
        remote(ref, ref, pair_send.at[0], recv_sem, partner).wait_recv()

    barrier = pltpu.get_barrier_semaphore()

    def greet(target_section, target):
        pl.semaphore_signal(
            barrier, inc=1, device_id=(target_section, target), device_id_type=MESH
        )

    greet(section, partner)
    for other in OTHERS:
        greet(section, 2 * chip(*other) + core)
    lax.fori_loop(1, sections, lambda i, c: (greet((section + i) % sections, me), c)[1], 0)

    @pl.when(section == 0)
    def _():
        def one(i, carry):
            m, q = i // CHIPS, i % CHIPS
            pltpu.make_async_copy(
                inbound.at[m, :, span(q)], all_x.at[m, q], local_sem.at[0]
            ).start()
            return carry

        lax.fori_loop(0, CORES * CHIPS, one, 0)
        pltpu.make_async_copy(
            inbound.at[core, :, span(here)], x_buf.at[here], local_sem.at[1]
        ).start()

    @pl.when(section == encoders)
    def _():
        def one(q, carry):
            pltpu.make_async_copy(
                decoder.at[core, :, span(q)], x_buf.at[q], local_sem.at[1]
            ).start()
            return carry

        lax.fori_loop(0, CHIPS, one, 0)

    projections = (w_query, w_key, w_value)
    own_weights = [
        pltpu.make_async_copy(w.at[0], weights.at[p, core], local_sem.at[2 + p])
        for p, w in enumerate(projections)
    ]
    own_out_weights = pltpu.make_async_copy(w_out.at[0], out_weights.at[core], local_sem.at[5])
    for copy in own_weights:
        copy.start()
    own_out_weights.start()
    row = lax.broadcasted_iota(jnp.int32, sharp.shape[1:], 0)
    filled = jnp.zeros(sharp.shape[1:], F32)
    for h in range(heads):
        filled = jnp.where(row == h, sharpness[0, h] * (1.0 / head_size**0.5), filled)
    sharp[core] = filled

    give = [
        remote(w.at[0], weights.at[p, core], pair_send.at[p], pair_recv.at[p], partner)
        for p, w in enumerate(projections)
    ]
    give_out = remote(
        w_out.at[0], out_weights.at[core], pair_send.at[3], pair_recv.at[3], partner
    )
    give_sharp = remote(sharp.at[core], sharp.at[core], pair_send.at[4], pair_recv.at[4], partner)
    give_mix = remote(mix_out, mix_buf.at[core], pair_send.at[5], pair_recv.at[5], partner)

    def spread(buf, recv, send, u):
        ref = buf.at[here, piece(u)]
        return [
            remote(ref, ref, send.at[u, i], recv.at[u, here], 2 * chip(*other) + core)
            for i, other in enumerate(OTHERS)
        ]

    def arrive(buf, recv, u, q):
        landed(buf.at[q, piece(u)], recv.at[u, q])

    def enter(buf, recv, send):
        for u in range(SUB):
            arrive(buf, recv, u, here)
            for copy in spread(buf, recv, send, u):
                copy.start()

    def fold(block):
        square = block * block
        return square[:, :width] + square[:, width:]

    def project(buf, recv, gains, wanted, gathered):
        for step, other in enumerate(((0, 0),) + OTHERS):
            q = chip(*other)
            if gathered and step > 0:
                for u in range(SUB):
                    arrive(buf, recv, u, q)
            block = buf[q].astype(F32)
            squares[...] = fold(block) if step == 0 else squares[...] + fold(block)
            scaled = (block * gains[:, span(q)]).astype(BF16)
            for p in wanted:
                for side in range(CORES):
                    product = jnp.dot(
                        scaled, weights[p, side, span(q)], preferred_element_type=F32
                    )
                    acc[p, side] = product if step == 0 else acc[p, side] + product
        factor = row_factor()
        for p in wanted:
            for side in range(CORES):
                keep(p, side, acc[p, side] * factor)

    def project_local(m):
        for q in range(CHIPS):
            block = all_x[m, q].astype(F32)
            squares[...] = fold(block) if q == 0 else squares[...] + fold(block)
            scaled = (block * gain[:, span(q)]).astype(BF16)
            for p in (QUERY, KEY, VALUE):
                product = jnp.dot(scaled, weights[p, core, span(q)], preferred_element_type=F32)
                acc[p, 0] = product if q == 0 else acc[p, 0] + product
        factor = row_factor()
        for p in (QUERY, KEY, VALUE):
            keep(p, core, acc[p, 0] * factor)

    def row_factor():
        return lax.rsqrt(
            jnp.sum(squares[...], axis=1, keepdims=True) * (1.0 / features) + EPS
        )

    def keep(p, side, total):
        if p == QUERY:
            q_unit[side] = unit(total)
        elif p == KEY:
            k_unit[side] = unit(total)
        else:
            v_rows[side] = total.astype(BF16)

    def unit(projected):
        square = projected * projected
        upper = square.astype(BF16)
        lower = (square - upper.astype(F32)).astype(BF16)
        row = lax.broadcasted_iota(jnp.int32, (width, width), 0) // head_size
        column = lax.broadcasted_iota(jnp.int32, (width, width), 1) // head_size
        same = jnp.where(row == column, 1.0 / head_size, 0.0).astype(BF16)
        mean = jnp.dot(upper, same, preferred_element_type=F32) + jnp.dot(
            lower, same, preferred_element_type=F32
        )
        return (projected * lax.rsqrt(mean + EPS)).astype(BF16)

    def attend(side):
        queries = q_unit[side].astype(F32)
        keys = k_unit[side]
        values = v_rows[side]
        lane_head = lax.broadcasted_iota(jnp.int32, (length, width), 1) // head_size
        stacked = jnp.concatenate(
            [jnp.where(lane_head == h, queries, 0.0).astype(BF16) for h in range(heads)], axis=0
        )
        scores = lax.dot_general(
            stacked, keys, (((1,), (1,)), ((), ())), preferred_element_type=F32
        )
        mixture = jnp.zeros((length, width), F32)
        for h in range(heads):
            grown = jnp.exp(scores[h * length : (h + 1) * length] * sharp[side, pl.ds(h, 1)])
            total = jnp.sum(grown, axis=1, keepdims=True)
            share = (grown * (1.0 / total)).astype(BF16)
            mixed = jnp.dot(share, values, preferred_element_type=F32)
            mixture = jnp.where(lane_head == h, mixed, mixture)
        return mixture.astype(BF16)

    def partial(u, i):
        q = chip(*OTHERS[i])
        return remote(
            part_buf.at[q, piece(u)],
            sum_buf.at[here, piece(u)],
            sum_send.at[u, i],
            sum_recv.at[u, here],
            2 * q + core,
        )

    def project_out():
        mixture = [mix_buf[side] for side in range(CORES)]

        def product(q):
            return sum(
                jnp.dot(mixture[side], out_weights[side, :, span(q)], preferred_element_type=F32)
                for side in range(CORES)
            )

        for i, other in enumerate(OTHERS):
            q = chip(*other)
            part_buf[q] = product(q).astype(BF16)
            partial(0, i).start()
        for u in range(1, SUB):
            for i in range(CHIPS - 1):
                partial(u, i).start()
        part_buf[here] = product(here).astype(BF16)

    def onward(u):
        return pltpu.make_async_remote_copy(
            src_ref=own_out.at[piece(u)],
            dst_ref=x_buf.at[here, piece(u)],
            send_sem=next_send.at[u, 0],
            recv_sem=x_recv.at[u, here],
            device_id=(section + 1, me),
            device_id_type=MESH,
        )

    def to_memory(u, i):
        return pltpu.make_async_remote_copy(
            src_ref=own_out.at[piece(u)],
            dst_ref=mem_buf.at[here, piece(u)],
            send_sem=next_send.at[u, i],
            recv_sem=mem_recv.at[u, here],
            device_id=(encoders + i, me),
            device_id_type=MESH,
        )

    def share(u, i):
        target = 2 * chip(*OTHERS[i]) + core if i < CHIPS - 1 else partner
        return remote(
            own_out.at[piece(u)],
            cell(core, u, here),
            out_send.at[u, i],
            out_recv.at[core, u, here],
            target,
        )

    def hand(u, i):
        q = chip(*OTHERS[i])
        ref = cell(core, u, q)
        return remote(ref, ref, out_send.at[u, CHIPS + i], out_recv.at[core, u, q], partner)

    def share_begin(u):
        for i in range(CHIPS):
            share(u, i).start()

    def reduce():
        for u in range(SUB):
            at = piece(u)
            total = x_buf[here, at].astype(F32) + part_buf[here, at].astype(F32)
            for other in OTHERS:
                q = chip(*other)
                arrive(sum_buf, sum_recv, u, q)
                total = total + sum_buf[q, at].astype(F32)
            rounded = total.astype(BF16)
            own_out[at] = rounded

            @pl.when((section < sections - 1) & (section != encoders - 1))
            def _():
                onward(u).start()

            @pl.when(section == encoders - 1)
            def _():
                for i in range(sections - encoders):
                    to_memory(u, i).start()

            @pl.when(section == sections - 1)
            def _():
                share_begin(u)

            result[0, core, at, span(here)] = rounded

    @pl.when(section == 0)
    def _():
        pltpu.make_async_copy(all_x, all_x, local_sem.at[0]).wait()

    for copy in own_weights:
        copy.wait()

    def local_mixture(m):
        project_local(m)
        mixture = attend(core)

        @pl.when(core == m)
        def _():
            mix_buf[core] = mixture

        @pl.when(core != m)
        def _():
            mix_out[...] = mixture

    pl.when(section == 0)(lambda: local_mixture(0))

    pl.semaphore_wait(barrier, CHIPS + sections - 1)

    @pl.when((section == 0) & (core != 0))
    def _():
        give_mix.start()

    give_out.start()
    give_sharp.start()

    @pl.when(section > 0)
    def _():
        for copy in give:
            copy.start()

    own_out_weights.wait()

    @pl.when(section == 0)
    def _():
        pltpu.make_async_copy(
            inbound.at[core, :, span(here)], x_buf.at[here], local_sem.at[1]
        ).wait()
        give_out.wait_recv()

        @pl.when(core == 0)
        def _():
            landed(mix_buf.at[1 - core], pair_recv.at[5])
            project_out()

        local_mixture(1)

        @pl.when(core == 0)
        def _():
            reduce()
            give_mix.start()

        @pl.when(core != 0)
        def _():
            landed(mix_buf.at[1 - core], pair_recv.at[5])
            pl.delay(13000)
            project_out()
            reduce()

        give_sharp.wait_recv()

    @pl.when(section > 0)
    def _():
        give_sharp.wait_recv()
        for copy in give:
            copy.wait_recv()
        everything, context = (QUERY, KEY, VALUE), (KEY, VALUE)

        @pl.when(section == encoders)
        def _():
            pltpu.make_async_copy(x_buf, x_buf, local_sem.at[1]).wait()
            project(x_buf, x_recv, gain, (QUERY,), False)
            enter(mem_buf, mem_recv, mem_send)
            project(mem_buf, mem_recv, last_gain, context, True)

        @pl.when(section > encoders)
        def _():
            enter(mem_buf, mem_recv, mem_send)
            project(mem_buf, mem_recv, last_gain, context, True)
            enter(x_buf, x_recv, x_send)
            project(x_buf, x_recv, gain, (QUERY,), True)

        @pl.when(section < encoders)
        def _():
            enter(x_buf, x_recv, x_send)
            project(x_buf, x_recv, gain, everything, True)

        for side in range(CORES):
            mix_buf[side] = attend(side)
        give_out.wait_recv()
        project_out()
        reduce()

    @pl.when(section < sections - 1)
    def _():
        for u in range(SUB):
            share_begin(u)

    for u in range(SUB):
        for i, other in enumerate(OTHERS):
            q = chip(*other)
            landed(cell(core, u, q), out_recv.at[core, u, q])
            hand(u, i).start()
    for u in range(SUB):
        for other in ((0, 0),) + OTHERS:
            q = chip(*other)
            landed(cell(1 - core, u, q), out_recv.at[1 - core, u, q])

    give_out.wait_send()
    give_sharp.wait_send()
    pl.when(section == 0)(lambda: give_mix.wait_send())

    @pl.when(section > 0)
    def _():
        for copy in give:
            copy.wait_send()

    for u in range(SUB):
        for i in range(CHIPS - 1):
            partial(u, i).wait_send()
            hand(u, i).wait_send()
        for i in range(CHIPS):
            share(u, i).wait_send()

        @pl.when(section >= encoders)
        def _():
            for copy in spread(mem_buf, mem_recv, mem_send, u):
                copy.wait_send()

        @pl.when((section > 0) & (section != encoders))
        def _():
            for copy in spread(x_buf, x_recv, x_send, u):
                copy.wait_send()

        @pl.when((section < sections - 1) & (section != encoders - 1))
        def _():
            onward(u).wait_send()

        @pl.when(section == encoders - 1)
        def _():
            for i in range(sections - encoders):
                to_memory(u, i).wait_send()


def solution(mesh):
    sections, seq = mesh.shape["section"], mesh.shape["seq"]

    def shards(inbound, decoder, w_query, w_key, w_value, w_out, gain, sharpness, last_gain):
        batches, length, features = inbound.shape
        width = features // seq
        wide = CORES * width
        dma = pltpu.SemaphoreType.DMA
        blocks = pltpu.VMEM((CHIPS, length, wide), BF16)
        planes = pltpu.VMEM((CORES, length, width), BF16)
        outside = pl.BlockSpec(memory_space=pltpu.HBM)
        vmem = pl.BlockSpec(memory_space=pltpu.VMEM)
        return pl.pallas_call(
            kernel,
            out_shape=jax.ShapeDtypeStruct((1, batches, length, features), BF16),
            in_specs=[outside] * 6 + [vmem, pl.BlockSpec(memory_space=pltpu.SMEM), vmem],
            out_specs=vmem,
            scratch_shapes=[
                pltpu.VMEM((3, CORES, features, width), BF16),
                pltpu.VMEM((CORES, width, features), BF16),
                pltpu.VMEM((batches, CHIPS, length, wide), BF16),
                blocks,
                blocks,
                planes,
                pltpu.VMEM((length, width), BF16),
                blocks,
                blocks,
                pltpu.VMEM((length, wide), BF16),
                pltpu.VMEM((3, CORES, length, width), F32),
                pltpu.VMEM((length, width), F32),
                planes,
                planes,
                planes,
                pltpu.VMEM((CORES, 8, length), F32),
                dma((SUB, CHIPS)),
                dma((SUB, CHIPS)),
                dma((SUB, CHIPS)),
                dma((CORES, SUB, CHIPS)),
                dma((SUB, CHIPS - 1)),
                dma((SUB, CHIPS - 1)),
                dma((SUB, CHIPS - 1)),
                dma((SUB, 2 * CHIPS)),
                dma((SUB, sections)),
                dma((6,)),
                dma((6,)),
                dma((6,)),
            ],
            compiler_params=pltpu.CompilerParams(
                collective_id=0, has_side_effects=True, vmem_limit_bytes=60 * 1024 * 1024
            ),
            name="cascade",
        )(
            inbound,
            decoder,
            w_query,
            w_key,
            w_value,
            w_out,
            gain,
            sharpness,
            last_gain.reshape(1, features),
        )

    return jax.shard_map(
        shards,
        mesh=mesh,
        in_specs=(
            P(),
            P(),
            P("section", None, "seq"),
            P("section", None, "seq"),
            P("section", None, "seq"),
            P("section", "seq", None),
            P("section", None),
            P("section", "seq"),
            P(),
        ),
        out_specs=P("section", None, None, None),
        check_vma=False,
    )
```
